256 devices in a mesh: dp: 8 (over x, core), expert: 32 (over y, z).
Axes of the slice: x: 4, y: 4, z: 8, core: 2. Of those that a mesh axis runs over, the one named last changes fastest.
Arguments:
- out_grads: bfloat16 [32768, 3584], P(('dp', 'expert')), may hold values from -6 to 6
- route_probs: float32 [32768, 4], P(('dp', 'expert')), may hold values from 0.05 to 1
- expert_ids: int32 [32768, 4], P(('dp', 'expert')), may hold values from 0 to 31, all different within a row; in each aligned block of 128 rows (0 to 127, 128 to 255, ...) at most 24 rows name the same one
- saved_inputs: bfloat16 [32768, 4, 1024], P(('dp', 'expert')), may hold values from -0.59765625 to 0.59765625
- w_latent: bfloat16 [32, 3584, 1024], P('expert'), as said below
- block_exponents: int32 [32, 3584, 8], P('expert'), may hold values from -9 to -6, as said below
Outputs:
- input_grads: bfloat16 [32768, 4, 1024], P(('dp', 'expert'))
- weight_grads: float32 [32, 3584, 1024], P('expert', 'dp')
The draws below stay inside these ranges and needn't reach their ends.
Inputs may be any that keep to these rules, and one draw needn't show every extreme that they name: `expert_ids`: each token names 4 different experts; the 128 tokens of one device name one expert in at most 24 slots, and some expert reaches 24. `block_exponents`: one exponent per 128 consecutive inputs of one output feature. w_latent * 2^(-exponent) lies within 0.45 of a whole number from -9 to 8.
All inputs are finite; a program needn't handle non-finite values.
Results may differ from the reference program's by a relative error of at most 0.012.
Values may be sent and summed in bfloat16 or wider, within the bound.
No kernel may reach another device: no remote copies, remote signals or barrier semaphores. Data moves between devices by JAX's collectives and lax.ppermute only.
A program may use at most 128 MiB of HBM per device.

```python
import math
import jax
import jax.numpy as jnp
import numpy as np
from jax import lax

D = 3584
FF = 1024
BLK = 128
TOPK = 4
TOK_DEV = 128
EXPERTS = 32
CAP = 24
TOKENS = 32768
N_DP = 8
N_EXPERT = 32


def weight_parts(key):
    base = jax.random.fold_in(key, 7001)
    exponents = jax.random.randint(jax.random.fold_in(base, 1), (EXPERTS, D, FF // BLK), -9, -5)
    levels = jax.random.randint(jax.random.fold_in(base, 2), (EXPERTS, D, FF), -9, 9)
    return (exponents.astype(jnp.int32), levels, base)


def draw_block_exponents(key, part):
    exponents, levels, base = weight_parts(key)
    return exponents


def draw_w_latent(key, part):
    exponents, levels, base = weight_parts(key)
    offsets = jax.random.uniform(jax.random.fold_in(base, 3), (EXPERTS, D, FF), jnp.float32, -0.3, 0.3)
    shifts = jnp.repeat(-exponents, BLK, axis=2)
    powers = jnp.left_shift(jnp.ones_like(shifts), shifts).astype(jnp.float32)
    return ((levels.astype(jnp.float32) + offsets) / powers).astype(jnp.bfloat16)


def level_of(key, shape, pieces, least, top_value):
    loudness = 1.0
    for dim, parts in pieces:
        steps = jax.random.uniform(jax.random.fold_in(jax.random.fold_in(key, 6), dim), (parts,), jnp.float32, least / len(pieces), top_value / len(pieces))
        loudness = loudness * jnp.repeat(jnp.exp(steps), shape[dim] // parts).reshape((-1,) + (1,) * (len(shape) - 1 - dim))
    return loudness


def routed_block(own_key, own, number, rows, count, top, most, lean):
    sequence = jax.random.permutation(own_key, count)
    crowded, ordinary = shares(count, rows * top, most, lean, True), shares(count, rows * top, most, lean, False)
    places = jnp.arange(count)

    def named(lengths, rotation):
        used = int((lengths > 0).sum())
        fixed = max(1, used // 4)
        moved = fixed + (places - fixed + rotation * (used - fixed)) % max(1, count - fixed)
        return jnp.zeros((count,), jnp.int32).at[sequence[jnp.where(places < fixed, places, moved)]].set(jnp.asarray(lengths, jnp.int32))

    lengths = jnp.where(number % 4 == 0, named(crowded, number // 4), named(ordinary, number - number // 4 - 1))
    mixed = jax.random.permutation(jax.random.fold_in(own, 3), count)
    donor, taker = mixed[0:count // 2 * 2:2], mixed[1:count // 2 * 2:2]
    slack = jnp.minimum(lengths[donor] - 1, most - lengths[taker]) // 2
    slack = jnp.where((donor == sequence[0]) | (taker == sequence[0]) | (lengths[taker] == 0), 0, jnp.maximum(slack, 0))
    moved = jax.random.randint(jax.random.fold_in(own, 4), (count // 2,), 0, 1 << 20) % (slack + 1)
    lengths = lengths.at[donor].add(-moved).at[taker].add(moved)
    members = jnp.searchsorted(jnp.cumsum(lengths), jnp.arange(rows * top), side="right").astype(jnp.int32)
    grid = members.reshape(top, rows).T
    grid = grid[jax.random.permutation(jax.random.fold_in(own, 1), rows)]
    rotation = jax.random.randint(jax.random.fold_in(own, 2), (rows, 1), 0, top)
    return jnp.take_along_axis(grid, (jnp.arange(top)[None, :] + rotation) % top, axis=1)


def shares(amount, total, bound, lean, full):
    portions = [(1 << 20) // math.isqrt(standing ** lean) + 1 for standing in range(1, amount + 1)]
    largest = bound if full else min(bound, max(-(-total // amount), total * portions[0] // sum(portions)))
    least = 1 if total - largest >= amount - 1 else 0
    given, surplus = [largest] + [least] * (amount - 1), total - largest - least * (amount - 1)
    while surplus > 0:
        movable = [i for i in range(1, amount) if given[i] < largest] or [i for i in range(1, amount) if given[i] < bound]
        whole, budget = sum([portions[i] for i in movable]), surplus
        for i in movable:
            addition = min(bound - given[i], max(1, budget * portions[i] // whole), surplus)
            given[i] = given[i] + addition
            surplus = surplus - addition
    return np.array(given)


def normal_values(stream_key, extent, spread, limit, shards=(), kind=jnp.bfloat16):
    factor_of = level_of(stream_key, extent, shards, -0.22, 0.18) if shards else 1.0
    array = jax.random.normal(stream_key, extent, jnp.float32) * spread * factor_of
    return jnp.minimum(jnp.maximum(array, -limit), limit).astype(kind)


def setup_inputs(seed: int = 0) -> dict:
    keys = jax.random.split(jax.random.key(seed), 7)
    out_grads = normal_values(keys[0], (TOKENS, D), 1.0, 6.0, ((0, 256),))
    route_probs = jnp.clip(jnp.exp(math.log(1.0) - 2.9957323 * jax.random.uniform(keys[1], (TOKENS, TOPK), jnp.float32) ** level_of(keys[1], (TOKENS, TOPK), ((0, 256),), -0.2, 0.2)), 0.05, 1.0)
    expert_ids_keys = jax.random.split(jax.random.fold_in(keys[2], 1), TOKENS // TOK_DEV)
    expert_ids_turns = jax.random.permutation(jax.random.fold_in(keys[2], 3), TOKENS // TOK_DEV)
    expert_ids = jax.vmap(lambda own, number: routed_block(jax.random.fold_in(keys[2], 2), own, number, TOK_DEV, EXPERTS, TOPK, CAP, 2))(expert_ids_keys, expert_ids_turns).reshape((TOKENS, TOPK))
    saved_inputs = normal_values(keys[3], (TOKENS, TOPK, FF), 0.1, 0.59765625, ((0, 256),))
    w_latent = draw_w_latent(jax.random.fold_in(keys[6], 71), 0)
    block_exponents = draw_block_exponents(jax.random.fold_in(keys[6], 71), 0)
    return {"out_grads": out_grads, "route_probs": route_probs, "expert_ids": expert_ids, "saved_inputs": saved_inputs, "w_latent": w_latent, "block_exponents": block_exponents}


def dequantize(weight_one, exponent_one):
    shifts = jnp.repeat(-exponent_one, BLK, axis=1)
    powers = jnp.left_shift(jnp.ones_like(shifts), shifts).astype(jnp.float32)
    codes = weight_one.astype(jnp.float32) * powers
    levels = jnp.clip(jnp.floor(codes + 0.5), -8.0, 7.0)
    quantized = (levels / powers).astype(jnp.bfloat16)
    inside = ((codes >= -8.5) & (codes <= 7.5)).astype(jnp.float32)
    return quantized, inside


def reference(out_grads, route_probs, expert_ids, saved_inputs, w_latent, block_exponents):
    slot_total = TOKENS * TOPK
    per_device = TOK_DEV * TOPK
    slot_room = N_EXPERT * CAP
    flat_ids = expert_ids.reshape(-1).astype(jnp.int32)
    grouped = flat_ids.reshape(-1, per_device)
    onehot = (grouped[:, :, None] == jnp.arange(EXPERTS, dtype=jnp.int32)[None, None, :]).astype(jnp.int32)
    before = jnp.cumsum(onehot, axis=1) - onehot
    position = jnp.sum(before * onehot, axis=2).reshape(-1).astype(jnp.int32)
    slot_ids = jnp.arange(slot_total, dtype=jnp.int32)
    device = slot_ids // per_device
    replica = device // N_EXPERT
    source = device % N_EXPERT
    target = (((flat_ids * N_DP + replica) * N_EXPERT + source) * CAP + position).astype(jnp.int32)
    table = jnp.full((EXPERTS * N_DP * slot_room,), slot_total, jnp.int32).at[target].set(slot_ids)
    table = table.reshape(EXPERTS, N_DP, slot_room)
    flat_probs = route_probs.reshape(-1)
    flat_inputs = saved_inputs.reshape(slot_total, FF)

    def one_expert(packed):
        weight_one, exponent_one, rows_all = packed
        quantized, inside = dequantize(weight_one, exponent_one)

        def one_replica(summed, row_ids):
            live = row_ids < slot_total
            safe = jnp.minimum(row_ids, slot_total - 1)
            weights_here = jnp.where(live, flat_probs[safe], jnp.zeros((), jnp.float32))
            grads = (weights_here[:, None] * out_grads[safe // TOPK].astype(jnp.float32)).astype(jnp.bfloat16)
            inputs_here = jnp.where(live[:, None], flat_inputs[safe], jnp.zeros((), jnp.bfloat16))
            back = jnp.dot(grads, quantized, preferred_element_type=jnp.float32).astype(jnp.bfloat16)
            partial_sum = lax.dot_general(grads, inputs_here, (((0,), (0,)), ((), ())), preferred_element_type=jnp.float32)
            rounded = lax.optimization_barrier(partial_sum.astype(jnp.bfloat16)).astype(jnp.float32)
            return summed + rounded, back

        summed, backs = lax.scan(one_replica, jnp.zeros((D, FF), jnp.float32), rows_all)
        return inside * summed, backs

    weight_grads, backs = lax.map(one_expert, (w_latent, block_exponents, table))
    input_grads = jnp.zeros((slot_total + 1, FF), jnp.bfloat16).at[table.reshape(-1)].set(backs.reshape(-1, FF))
    input_grads = input_grads[:slot_total].reshape(TOKENS, TOPK, FF)
    return input_grads, weight_grads
```

```python
import jax
import jax.numpy as jnp
from jax import lax
from jax.sharding import Mesh, PartitionSpec as P

BLK = 128
CHUNKS = 4


def dequantize(weight_one, exponent_one):
    shifts = jnp.repeat(-exponent_one, BLK, axis=1)
    powers = jnp.left_shift(jnp.ones_like(shifts), shifts).astype(jnp.float32)
    codes = weight_one.astype(jnp.float32) * powers
    levels = jnp.clip(jnp.floor(codes + 0.5), -8.0, 7.0)
    return (levels / powers).astype(jnp.bfloat16)


def kept(weight_one, exponent_one):
    shifts = jnp.repeat(-exponent_one, BLK, axis=1)
    powers = jnp.left_shift(jnp.ones_like(shifts), shifts).astype(jnp.float32)
    codes = weight_one.astype(jnp.float32) * powers
    return ((codes >= -8.5) & (codes <= 7.5)).astype(jnp.float32)


def local(out_grads, route_probs, expert_ids, saved_inputs, w_latent, block_exponents):
    ny, nz = lax.axis_size("y"), lax.axis_size("z")
    experts = ny * nz
    tok, topk = expert_ids.shape
    feat = out_grads.shape[1]
    hidden = saved_inputs.shape[2]
    cap = tok * topk * 3 // (2 * experts)
    slots = tok * topk
    rows = experts * cap
    width = feat // CHUNKS
    z = lax.axis_index("z")

    gathered = [
        lax.all_gather(out_grads[:, c * width : (c + 1) * width], "z", axis=0, tiled=False)
        for c in range(CHUNKS)
    ]
    small = jnp.concatenate([route_probs, expert_ids.astype(jnp.float32)], axis=1)
    small = lax.all_gather(small.T, "z", axis=0, tiled=False)
    probs_z = small[:, :topk, :]
    ids_z = small[:, topk:, :].astype(jnp.int32)

    flat_ids = expert_ids.reshape(slots)
    onehot = flat_ids[:, None] == jnp.arange(experts, dtype=jnp.int32)[None, :]
    tri = (jnp.arange(slots)[:, None] > jnp.arange(slots)[None, :]).astype(jnp.bfloat16)
    before = jnp.dot(tri, onehot.astype(jnp.bfloat16), preferred_element_type=jnp.float32)
    position = jnp.sum(jnp.where(onehot, before, 0.0), axis=1).astype(jnp.int32)
    target = flat_ids * cap + position
    place = (jnp.arange(rows, dtype=jnp.int32)[:, None] == target[None, :]).astype(jnp.bfloat16)
    send_inputs = jnp.dot(
        place, saved_inputs.reshape(slots, hidden), preferred_element_type=jnp.float32
    ).astype(jnp.bfloat16)
    got_inputs = lax.all_to_all(
        send_inputs.reshape(experts, cap, hidden),
        ("y", "z"), split_axis=0, concat_axis=0, tiled=True,
    ).reshape(rows, hidden)

    mine = jnp.arange(ny, dtype=jnp.int32) * nz + z
    hit = ids_z[None] == mine[:, None, None, None]
    there = jnp.any(hit, axis=2)
    prob = jnp.sum(jnp.where(hit, probs_z[None], 0.0), axis=2)
    upper = (jnp.arange(tok)[:, None] < jnp.arange(tok)[None, :]).astype(jnp.bfloat16)
    order = jnp.einsum(
        "yzt,tu->yzu", there.astype(jnp.bfloat16), upper, preferred_element_type=jnp.float32
    ).astype(jnp.int32)
    chosen = there[:, :, None, :] & (order[:, :, None, :] == jnp.arange(cap)[None, None, :, None])
    slot_prob = jnp.sum(jnp.where(chosen, prob[:, :, None, :], 0.0), axis=3)
    chosen = chosen.astype(jnp.bfloat16)

    quantized = dequantize(w_latent[0], block_exponents[0])
    back = jnp.zeros((rows, hidden), jnp.float32)
    parts = []
    for c in range(CHUNKS):
        picked = jnp.einsum(
            "yzct,ztf->yzcf", chosen, gathered[c], preferred_element_type=jnp.float32
        )
        picked = (picked * slot_prob[..., None]).astype(jnp.bfloat16)
        got = lax.all_to_all(
            picked.reshape(ny, nz * cap, width), "y", split_axis=0, concat_axis=0, tiled=True
        ).reshape(rows, width)
        back = back + jnp.dot(
            got, quantized[c * width : (c + 1) * width], preferred_element_type=jnp.float32
        )
        parts.append(
            lax.dot_general(
                got, got_inputs, (((0,), (0,)), ((), ())), preferred_element_type=jnp.float32
            ).astype(jnp.bfloat16)
        )
    returned = lax.all_to_all(
        back.astype(jnp.bfloat16).reshape(experts, cap, hidden),
        ("y", "z"), split_axis=0, concat_axis=0, tiled=True,
    ).reshape(rows, hidden)
    input_grads = jnp.dot(place.T, returned, preferred_element_type=jnp.float32).astype(
        jnp.bfloat16
    )
    summed = lax.psum_scatter(
        jnp.concatenate(parts, axis=0), ("x", "core"), scatter_dimension=0, tiled=True
    ).astype(jnp.float32)
    share = feat // (lax.axis_size("x") * lax.axis_size("core"))
    at = (lax.axis_index("x") * lax.axis_size("core") + lax.axis_index("core")) * share
    keep_rows = kept(
        lax.dynamic_slice_in_dim(w_latent[0], at, share, 0),
        lax.dynamic_slice_in_dim(block_exponents[0], at, share, 0),
    )
    return (input_grads.reshape(tok, topk, hidden), (summed * keep_rows)[None])


def solution(mesh):
    split = Mesh(mesh.devices.reshape(4, 2, 4, 8), ("x", "core", "y", "z"))
    every = ("x", "core", "y", "z")
    placed = (
        P(every, None),
        P(every, None),
        P(every, None),
        P(every, None, None),
        P(("y", "z"), None, None),
        P(("y", "z"), None, None),
    )
    return jax.shard_map(
        local,
        mesh=split,
        in_specs=placed,
        out_specs=(P(every, None, None), P(("y", "z"), ("x", "core"), None)),
        check_vma=False,
    )
```

```python
import functools

import jax
import jax.numpy as jnp
from jax import lax
from jax.experimental import pallas as pl
from jax.experimental.pallas import tpu as pltpu
from jax.sharding import Mesh, PartitionSpec as P


BLK = 128
KERNEL_VMEM = 20 << 20
META = 128


def dequantize_kernel(weight_ref, exponent_ref, out_ref):
    powers = jnp.left_shift(jnp.ones_like(exponent_ref[...]), -exponent_ref[...])
    powers = powers.astype(jnp.float32).T
    inverses = 1.0 / powers
    center = jnp.bfloat16(192.0)
    for b in range(powers.shape[1]):
        here = slice(b * BLK, (b + 1) * BLK)
        shape = (powers.shape[0], BLK)
        power = jnp.broadcast_to(powers[:, b : b + 1], shape).astype(jnp.bfloat16)
        inverse = jnp.broadcast_to(inverses[:, b : b + 1], shape).astype(jnp.bfloat16)
        shifted = weight_ref[:, here] * power + center
        shifted = jnp.clip(shifted, jnp.bfloat16(184.0), jnp.bfloat16(199.0))
        out_ref[:, here] = (shifted - center) * inverse


def dequantize(weight_one, exponent_one):
    feat, hidden = weight_one.shape
    step = 512
    return pl.pallas_call(
        dequantize_kernel,
        out_shape=pltpu.VMEM((feat, hidden), jnp.bfloat16),
        grid=(feat // step,),
        in_specs=[
            pl.BlockSpec((step, hidden), lambda i: (i, 0)),
            pl.BlockSpec((hidden // BLK, step), lambda i: (0, i)),
        ],
        out_specs=pl.BlockSpec((step, hidden), lambda i: (i, 0)),
        cost_estimate=pl.CostEstimate(
            flops=12 * feat * hidden, bytes_accessed=4 * feat * hidden, transcendentals=0
        ),
        compiler_params=pltpu.CompilerParams(vmem_limit_bytes=KERNEL_VMEM),
        name="dequantize",
    )(weight_one, exponent_one.T)


def kept(weight_one, exponent_one):
    shifts = jnp.repeat(-exponent_one, BLK, axis=1)
    powers = jnp.left_shift(jnp.ones_like(shifts), shifts).astype(jnp.float32)
    codes = weight_one.astype(jnp.float32) * powers
    return (codes >= -8.5) & (codes <= 7.5)


def pick_kernel(ny, nz, cap, topk, feat, halves, at_ref, *refs):
    refs, outs = refs[:-ny], refs[-ny:]
    sources = [refs] if halves else [(r,) for r in refs]
    tok = sum(r.shape[0] for r in sources[0])
    y0, z0 = at_ref[0], at_ref[1]

    def split(j):
        g = jnp.zeros_like(j)
        for d in range(1, ny):
            g = g + (j >= d * cap).astype(jnp.int32)
        return g, j - g * cap

    def expert(g):
        y = y0 + g
        return (jnp.where(y >= ny, y - ny, y) * nz + z0).astype(jnp.float32)

    lane = lax.broadcasted_iota(jnp.int32, (tok, META), 1)
    group, slot = split(lane)
    lane_expert, lane_slot = expert(group), slot.astype(jnp.float32)
    row_expert = expert(split(lax.broadcasted_iota(jnp.int32, (META, META), 0))[0])[:, :1]
    earlier = (
        lax.broadcasted_iota(jnp.int32, (tok, tok), 1)
        < lax.broadcasted_iota(jnp.int32, (tok, tok), 0)
    )
    earlier = earlier.astype(jnp.float32).astype(jnp.bfloat16)

    for i, parts in enumerate(sources):

        def columns(lo, hi):
            got = [p[:, lo:hi] for p in parts]
            return got[0] if len(got) == 1 else jnp.concatenate(got, axis=0)

        meta_low = columns(feat, feat + META)
        meta = meta_low.astype(jnp.float32)
        hit = jnp.zeros((tok, META), jnp.float32)
        for k in range(topk):
            hit = jnp.where(meta[:, k : k + 1] == lane_expert, 1.0, hit)
        hit = jnp.where(lane < ny * cap, hit, 0.0)
        before = jnp.dot(earlier, hit.astype(jnp.bfloat16), preferred_element_type=jnp.float32)
        chosen = jnp.where(before == lane_slot, hit, 0.0)
        chosen = chosen.T.astype(jnp.bfloat16)
        info = jnp.dot(chosen, meta_low, preferred_element_type=jnp.float32)
        prob = jnp.zeros((META, 1), jnp.float32)
        for k in range(topk):
            value = info[:, topk + k : topk + k + 1]
            value = value + info[:, 2 * topk + k : 2 * topk + k + 1]
            value = value + info[:, 3 * topk + k : 3 * topk + k + 1]
            prob = jnp.where(info[:, k : k + 1] == row_expert, value, prob)
        step = 512
        for lo in range(0, feat, step):
            rows = jnp.dot(chosen, columns(lo, lo + step), preferred_element_type=jnp.float32)
            rows = rows * prob
            for d in range(ny):
                outs[d][i, :, lo : lo + step] = rows[d * cap : (d + 1) * cap].astype(jnp.bfloat16)


def pick(at, sources, ny, nz, cap, topk, feat, halves=False):
    count = 1 if halves else len(sources)
    tok = sum(s.shape[0] for s in sources) // count
    vmem = pl.BlockSpec(memory_space=pltpu.VMEM)
    return pl.pallas_call(
        functools.partial(pick_kernel, ny, nz, cap, topk, feat, halves),
        out_shape=[jax.ShapeDtypeStruct((count, cap, feat), jnp.bfloat16)] * ny,
        in_specs=[pl.BlockSpec(memory_space=pltpu.SMEM)] + [vmem] * len(sources),
        out_specs=[vmem] * ny,
        cost_estimate=pl.CostEstimate(
            flops=2 * count * META * tok * feat,
            bytes_accessed=2 * count * (tok + ny * cap) * feat,
            transcendentals=0,
        ),
        compiler_params=pltpu.CompilerParams(vmem_limit_bytes=KERNEL_VMEM),
    )(at, *sources)


def wrapped(a, size):
    return jnp.where(a >= size, a - size, jnp.where(a < 0, a + size, a))


def chunk_sources(nz):
    return [[0, 1, -1]] + [[s, -s] for s in range(2, nz // 2)] + [[nz // 2]]


def to_absolute_kernel(ny, nz, cap, at_ref, *refs):
    out_ref = refs[-1]
    y0, z0 = at_ref[0], at_ref[1]
    for ref, distances in zip(refs[:-1], chunk_sources(nz), strict=True):
        for d in range(ny):
            for i, s in enumerate(distances):
                lo = (d * len(distances) + i) * cap
                out_ref[wrapped(y0 - d, ny), wrapped(z0 - s, nz)] = ref[lo : lo + cap, :]


def to_absolute(at, parts, ny, nz, cap):
    vmem = pl.BlockSpec(memory_space=pltpu.VMEM)
    width = parts[0].shape[1]
    return pl.pallas_call(
        functools.partial(to_absolute_kernel, ny, nz, cap),
        out_shape=jax.ShapeDtypeStruct((ny, nz, cap, width), jnp.bfloat16),
        in_specs=[pl.BlockSpec(memory_space=pltpu.SMEM)] + [vmem] * len(parts),
        out_specs=vmem,
        cost_estimate=pl.CostEstimate(
            flops=0, bytes_accessed=4 * ny * nz * cap * width, transcendentals=0
        ),
        compiler_params=pltpu.CompilerParams(vmem_limit_bytes=KERNEL_VMEM),
        name="to_absolute",
    )(at, *parts)


def to_relative_kernel(ny, nz, cap, at_ref, in_ref, out_ref):
    y0, z0 = at_ref[0], at_ref[1]
    lo = 0
    for distances in chunk_sources(nz):
        for d in range(ny):
            for s in distances:
                out_ref[lo : lo + cap, :] = in_ref[wrapped(y0 - d, ny), wrapped(z0 - s, nz)]
                lo += cap


def to_relative(at, a, ny, nz, cap):
    vmem = pl.BlockSpec(memory_space=pltpu.VMEM)
    width = a.shape[-1]
    return pl.pallas_call(
        functools.partial(to_relative_kernel, ny, nz, cap),
        out_shape=jax.ShapeDtypeStruct((ny * nz * cap, width), jnp.bfloat16),
        in_specs=[pl.BlockSpec(memory_space=pltpu.SMEM), vmem],
        out_specs=vmem,
        cost_estimate=pl.CostEstimate(
            flops=0, bytes_accessed=4 * ny * nz * cap * width, transcendentals=0
        ),
        compiler_params=pltpu.CompilerParams(vmem_limit_bytes=KERNEL_VMEM),
        name="to_relative",
    )(at, a.reshape(ny, nz, cap, width))


def shift(a, axis, size, by):
    return lax.ppermute(a, axis, [(i, (i + by) % size) for i in range(size)])


def local(out_grads, route_probs, expert_ids, saved_inputs, w_latent, block_exponents):
    nx, nc, ny, nz = (lax.axis_size(a) for a in ("x", "core", "y", "z"))
    experts = ny * nz
    tok, topk = expert_ids.shape
    feat = out_grads.shape[1]
    hidden = saved_inputs.shape[2]
    cap = tok * topk * 3 // (2 * experts)
    slots = tok * topk
    rows = experts * cap
    at = jnp.stack([lax.axis_index("y"), lax.axis_index("z")]).astype(jnp.int32)

    high = lax.reduce_precision(route_probs, 8, 7)
    rest = route_probs - high
    middle = lax.reduce_precision(rest, 8, 7)
    meta = jnp.concatenate(
        [expert_ids.astype(jnp.float32), high, middle, rest - middle], axis=1
    ).astype(jnp.bfloat16)
    meta = jnp.pad(meta, ((0, 0), (0, META - 4 * topk)))
    own = jnp.concatenate([out_grads, meta], axis=1)

    flat_ids = expert_ids.reshape(slots)
    onehot = flat_ids[:, None] == jnp.arange(experts, dtype=jnp.int32)[None, :]
    tri = (jnp.arange(slots)[:, None] > jnp.arange(slots)[None, :]).astype(jnp.bfloat16)
    before = jnp.dot(tri, onehot.astype(jnp.bfloat16), preferred_element_type=jnp.float32)
    position = jnp.sum(jnp.where(onehot, before, 0.0), axis=1).astype(jnp.int32)
    target = flat_ids * cap + position
    place = (jnp.arange(rows, dtype=jnp.int32)[:, None] == target[None, :]).astype(jnp.bfloat16)
    half = hidden // 2

    def dispatch(columns):
        return jnp.dot(place, columns, preferred_element_type=jnp.float32).astype(jnp.bfloat16)

    def exchange(a):
        return lax.all_to_all(
            a.reshape(experts, cap, a.shape[-1]), ("y", "z"), split_axis=0, concat_axis=0, tiled=True
        )

    flat_inputs = saved_inputs.reshape(slots, hidden)
    first = exchange(dispatch(flat_inputs[:, :half]))
    second = dispatch(flat_inputs[:, half:])
    quantized = dequantize(w_latent[0], block_exponents[0])

    share = feat // (nx * nc)
    core, x = lax.axis_index("core"), lax.axis_index("x")
    start = (x * nc + core) * share
    keep_rows = kept(
        lax.dynamic_slice_in_dim(w_latent[0], start, share, 0),
        lax.dynamic_slice_in_dim(block_exponents[0], start, share, 0),
    ).astype(jnp.bfloat16)

    got, backs = [], []

    def deliver(sources, halves=False):
        picked = pick(at, sources, ny, nz, cap, topk, feat, halves)
        pieces = [picked[0]]
        for d in range(1, ny):
            pieces.append(shift(picked[d], "y", ny, d))
        got.append(pieces)

    def finish(s):
        got[s] = jnp.concatenate(got[s], axis=0).reshape(-1, feat)
        backs.append(
            jnp.dot(got[s], quantized, preferred_element_type=jnp.float32).astype(
                jnp.bfloat16
            )
        )

    def hop(right, left):
        right = shift(right, "z", nz, 1)
        left = shift(left, "z", nz, -1)
        return right, left

    right, left = hop(own, own)
    right, left, second, keep_rows = lax.optimization_barrier((right, left, second, keep_rows))
    deliver([own, right, left])
    right, left = hop(right, left)
    right, left, first, quantized = lax.optimization_barrier((right, left, first, quantized))
    deliver([right, left])
    right, left = hop(right, left)
    finish(0)
    right, left, backs[0] = lax.optimization_barrier((right, left, backs[0]))
    deliver([right, left])
    right, left = hop(right[: tok // 2], left[tok // 2 :])
    second, right, left = lax.optimization_barrier((second, right, left))
    deliver([right, left], halves=True)
    second = exchange(second)
    for s in range(1, 4):
        finish(s)

    back = to_absolute(at, backs, ny, nz, cap)
    back, got = lax.optimization_barrier((back, got))
    returned = exchange(back).reshape(rows, hidden)
    input_grads = jnp.dot(place.T, returned, preferred_element_type=jnp.float32).astype(
        jnp.bfloat16
    )

    all_grads = jnp.concatenate(got, axis=0)

    def reduced(inputs, then=None):
        partial = lax.dot_general(
            all_grads,
            to_relative(at, inputs, ny, nz, cap),
            (((0,), (0,)), ((), ())),
            preferred_element_type=jnp.float32,
        ).astype(jnp.bfloat16)
        partial = partial.reshape(nx, nc, share, -1)
        other = lax.dynamic_index_in_dim(partial, 1 - core, 1, keepdims=False)
        mine = lax.dynamic_index_in_dim(partial, core, 1, keepdims=False)
        other = shift(other, "core", nc, 1)
        width = inputs.shape[-1] // 2

        def piece(d, columns=slice(None)):
            at_x = wrapped(x + d, nx)
            a = lax.dynamic_index_in_dim(mine, at_x, 0, keepdims=False)[:, columns]
            b = lax.dynamic_index_in_dim(other, at_x, 0, keepdims=False)[:, columns]
            return a.astype(jnp.float32) + b.astype(jnp.float32)

        low, high = slice(0, width), slice(width, None)
        up, down = piece(2, low).astype(jnp.bfloat16), piece(2, high).astype(jnp.bfloat16)
        up, down, then = lax.optimization_barrier((up, down, then))
        up, down = shift(up, "x", nx, 1), shift(down, "x", nx, -1)
        to_right = jnp.concatenate(
            [piece(1, low) + up.astype(jnp.float32), piece(1, high)], axis=1
        ).astype(jnp.bfloat16)
        to_left = jnp.concatenate(
            [piece(-1, low), piece(-1, high) + down.astype(jnp.float32)], axis=1
        ).astype(jnp.bfloat16)
        from_left = shift(to_right, "x", nx, 1).astype(jnp.float32)
        from_right = shift(to_left, "x", nx, -1).astype(jnp.float32)
        return piece(0) + from_left + from_right, then

    summed_first, second = reduced(first, second)
    summed_second, _ = reduced(second)
    summed = jnp.concatenate([summed_first, summed_second], axis=1)
    weight_grads = summed * keep_rows.astype(jnp.float32)
    return (input_grads.reshape(tok, topk, hidden), weight_grads[None])


def solution(mesh):
    split = Mesh(mesh.devices.reshape(4, 2, 4, 8), ("x", "core", "y", "z"))
    every = ("x", "core", "y", "z")
    placed = (
        P(every, None),
        P(every, None),
        P(every, None),
        P(every, None, None),
        P(("y", "z"), None, None),
        P(("y", "z"), None, None),
    )
    return jax.shard_map(
        local,
        mesh=split,
        in_specs=placed,
        out_specs=(P(every, None, None), P(("y", "z"), ("x", "core"), None)),
        check_vma=False,
    )
```

```python
import functools

import jax
import jax.numpy as jnp
from jax import lax
from jax.experimental import pallas as pl
from jax.experimental.pallas import tpu as pltpu
from jax.sharding import Mesh, PartitionSpec as P


BLK = 128
KERNEL_VMEM = 20 << 20
META = 128


def dequantize_kernel(weight_ref, exponent_ref, out_ref):
    powers = jnp.left_shift(jnp.ones_like(exponent_ref[...]), -exponent_ref[...])
    powers = powers.astype(jnp.float32).T
    inverses = 1.0 / powers
    center = jnp.bfloat16(192.0)
    for b in range(powers.shape[1]):
        here = slice(b * BLK, (b + 1) * BLK)
        shape = (powers.shape[0], BLK)
        power = jnp.broadcast_to(powers[:, b : b + 1], shape).astype(jnp.bfloat16)
        inverse = jnp.broadcast_to(inverses[:, b : b + 1], shape).astype(jnp.bfloat16)
        shifted = weight_ref[:, here] * power + center
        shifted = jnp.clip(shifted, jnp.bfloat16(184.0), jnp.bfloat16(199.0))
        out_ref[:, here] = (shifted - center) * inverse


def dequantize(weight_one, exponent_one):
    feat, hidden = weight_one.shape
    step = 256
    return pl.pallas_call(
        dequantize_kernel,
        out_shape=jax.ShapeDtypeStruct((feat, hidden), jnp.bfloat16),
        grid=(feat // step,),
        in_specs=[
            pl.BlockSpec((step, hidden), lambda i: (i, 0)),
            pl.BlockSpec((hidden // BLK, step), lambda i: (0, i)),
        ],
        out_specs=pl.BlockSpec((step, hidden), lambda i: (i, 0)),
        cost_estimate=pl.CostEstimate(
            flops=12 * feat * hidden, bytes_accessed=4 * feat * hidden, transcendentals=0
        ),
        compiler_params=pltpu.CompilerParams(vmem_limit_bytes=KERNEL_VMEM),
        name="dequantize",
    )(weight_one, exponent_one.T)


def kept_kernel(at_ref, weight_ref, exponent_ref, out_ref):
    powers = jnp.left_shift(jnp.ones_like(exponent_ref[...]), -exponent_ref[...])
    powers = powers.astype(jnp.float32)
    for b in range(powers.shape[1]):
        here = slice(b * BLK, (b + 1) * BLK)
        codes = weight_ref[:, here].astype(jnp.float32) * powers[:, b : b + 1]
        inside = jnp.where(codes >= -8.5, jnp.where(codes <= 7.5, 1.0, 0.0), 0.0)
        out_ref[:, here] = inside.astype(jnp.bfloat16)


def kept(block, weight_one, exponents, share):
    hidden = weight_one.shape[1]
    parts = 7
    step = share // parts
    return pl.pallas_call(
        kept_kernel,
        out_shape=jax.ShapeDtypeStruct((share, hidden), jnp.bfloat16),
        grid_spec=pltpu.PrefetchScalarGridSpec(
            num_scalar_prefetch=1,
            grid=(parts,),
            in_specs=[
                pl.BlockSpec((step, hidden), lambda i, at: (at[0] * parts + i, 0)),
                pl.BlockSpec((step, hidden // BLK), lambda i, at: (i, 0)),
            ],
            out_specs=pl.BlockSpec((step, hidden), lambda i, at: (i, 0)),
        ),
        cost_estimate=pl.CostEstimate(
            flops=4 * share * hidden, bytes_accessed=4 * share * hidden, transcendentals=0
        ),
        compiler_params=pltpu.CompilerParams(vmem_limit_bytes=KERNEL_VMEM),
        name="kept",
    )(block, weight_one, exponents)


def pieces_kernel(at_ref, mine_ref, other_ref, out_ref):
    total = mine_ref[0, 0].astype(jnp.float32) + other_ref[0].astype(jnp.float32)
    out_ref[0] = total.astype(jnp.bfloat16)


def pieces_of(at, partial, other):
    nx, _, share, width = partial.shape
    return pl.pallas_call(
        pieces_kernel,
        out_shape=jax.ShapeDtypeStruct((nx, share, width), jnp.bfloat16),
        grid_spec=pltpu.PrefetchScalarGridSpec(
            num_scalar_prefetch=1,
            grid=(nx,),
            in_specs=[
                pl.BlockSpec(
                    (1, 1, share, width), lambda d, at: (lax.rem(at[0] + d, nx), at[1], 0, 0)
                ),
                pl.BlockSpec((1, share, width), lambda d, at: (lax.rem(at[0] + d, nx), 0, 0)),
            ],
            out_specs=pl.BlockSpec((1, share, width), lambda d, at: (d, 0, 0)),
        ),
        cost_estimate=pl.CostEstimate(
            flops=nx * share * width, bytes_accessed=6 * nx * share * width, transcendentals=0
        ),
        name="pieces",
    )(at, partial, other)


def pick_kernel(ny, nz, cap, topk, feat, shape, at_ref, *refs):
    refs, outs = refs[:-ny], refs[-ny:]
    sources, lo = [], 0
    for parts in shape:
        sources.append(refs[lo : lo + parts])
        lo += parts
    tok = sum(r.shape[0] for r in sources[0])
    y0, z0 = at_ref[0], at_ref[1]

    def split(j):
        g = jnp.zeros_like(j)
        for d in range(1, ny):
            g = g + (j >= d * cap).astype(jnp.int32)
        return g, j - g * cap

    def expert(g):
        y = y0 + g
        return (jnp.where(y >= ny, y - ny, y) * nz + z0).astype(jnp.float32)

    lane = lax.broadcasted_iota(jnp.int32, (tok, META), 1)
    group, slot = split(lane)
    lane_expert, lane_slot = expert(group), slot.astype(jnp.float32)
    row_expert = expert(split(lax.broadcasted_iota(jnp.int32, (META, META), 0))[0])[:, :1]
    earlier = (
        lax.broadcasted_iota(jnp.int32, (tok, tok), 1)
        < lax.broadcasted_iota(jnp.int32, (tok, tok), 0)
    )
    earlier = earlier.astype(jnp.float32).astype(jnp.bfloat16)

    for i, parts in enumerate(sources):

        def columns(lo, hi):
            got = [p[:, lo:hi] for p in parts]
            return got[0] if len(got) == 1 else jnp.concatenate(got, axis=0)

        meta_low = columns(feat, feat + META)
        meta = meta_low.astype(jnp.float32)
        hit = jnp.zeros((tok, META), jnp.float32)
        for k in range(topk):
            hit = jnp.where(meta[:, k : k + 1] == lane_expert, 1.0, hit)
        hit = jnp.where(lane < ny * cap, hit, 0.0)
        before = jnp.dot(earlier, hit.astype(jnp.bfloat16), preferred_element_type=jnp.float32)
        chosen = jnp.where(before == lane_slot, hit, 0.0)
        chosen = chosen.T.astype(jnp.bfloat16)
        info = jnp.dot(chosen, meta_low, preferred_element_type=jnp.float32)
        prob = jnp.zeros((META, 1), jnp.float32)
        for k in range(topk):
            value = info[:, topk + k : topk + k + 1]
            value = value + info[:, 2 * topk + k : 2 * topk + k + 1]
            value = value + info[:, 3 * topk + k : 3 * topk + k + 1]
            prob = jnp.where(info[:, k : k + 1] == row_expert, value, prob)
        step = 512
        for lo in range(0, feat, step):
            rows = jnp.dot(chosen, columns(lo, lo + step), preferred_element_type=jnp.float32)
            rows = rows * prob
            for d in range(ny):
                outs[d][i, :, lo : lo + step] = rows[d * cap : (d + 1) * cap].astype(jnp.bfloat16)


def pick(at, sources, ny, nz, cap, topk, feat):
    count = len(sources)
    shape = tuple(len(parts) for parts in sources)
    tok = sum(p.shape[0] for p in sources[0])
    flat = [p for parts in sources for p in parts]
    vmem = pl.BlockSpec(memory_space=pltpu.VMEM)
    return pl.pallas_call(
        functools.partial(pick_kernel, ny, nz, cap, topk, feat, shape),
        out_shape=[jax.ShapeDtypeStruct((count, cap, feat), jnp.bfloat16)] * ny,
        in_specs=[pl.BlockSpec(memory_space=pltpu.SMEM)] + [vmem] * len(flat),
        out_specs=[vmem] * ny,
        cost_estimate=pl.CostEstimate(
            flops=2 * count * META * tok * feat,
            bytes_accessed=2 * count * (tok + ny * cap) * feat,
            transcendentals=0,
        ),
        compiler_params=pltpu.CompilerParams(vmem_limit_bytes=KERNEL_VMEM),
    )(at, *flat)


def wrapped(a, size):
    return jnp.where(a >= size, a - size, jnp.where(a < 0, a + size, a))


def chunk_sources(nz):
    return [[0, 1, -1]] + [[s, -s] for s in range(2, nz // 2)] + [[nz // 2]]


def multiply_kernel(*refs):
    pieces, (weight_ref, out_ref, rows_ref, acc_ref) = refs[:-4], refs[-4:]
    i = pl.program_id(0)
    rows = [p[c] for p in pieces for c in range(p.shape[0])]
    here = jnp.concatenate(rows, axis=0)
    rows_ref[...] = here
    part = jnp.dot(here, weight_ref[...], preferred_element_type=jnp.float32)

    @pl.when(i == 0)
    def _():
        acc_ref[...] = part

    @pl.when(i > 0)
    def _():
        acc_ref[...] += part

    @pl.when(i == pl.num_programs(0) - 1)
    def _():
        out_ref[...] = acc_ref[...].astype(jnp.bfloat16)


def multiply(pieces, weight):
    cap, feat = pieces[0].shape[1:]
    rows, hidden, step = sum(p.shape[0] for p in pieces) * cap, weight.shape[1], 256
    return pl.pallas_call(
        multiply_kernel,
        out_shape=[
            jax.ShapeDtypeStruct((rows, hidden), jnp.bfloat16),
            jax.ShapeDtypeStruct((rows, feat), jnp.bfloat16),
        ],
        grid=(feat // step,),
        in_specs=[pl.BlockSpec((p.shape[0], cap, step), lambda i: (0, 0, i)) for p in pieces]
        + [pl.BlockSpec((step, hidden), lambda i: (i, 0))],
        out_specs=[
            pl.BlockSpec((rows, hidden), lambda i: (0, 0)),
            pl.BlockSpec((rows, step), lambda i: (0, i)),
        ],
        scratch_shapes=[pltpu.VMEM((rows, hidden), jnp.float32)],
        cost_estimate=pl.CostEstimate(
            flops=2 * rows * feat * hidden,
            bytes_accessed=2 * feat * (rows + hidden),
            transcendentals=0,
        ),
        name="multiply",
    )(*pieces, weight)


def to_absolute_kernel(ny, nz, cap, at_ref, *refs):
    out_ref = refs[-1]
    y0, z0 = at_ref[0], at_ref[1]
    for ref, distances in zip(refs[:-1], chunk_sources(nz), strict=True):
        for d in range(ny):
            for i, s in enumerate(distances):
                lo = (d * len(distances) + i) * cap
                out_ref[wrapped(y0 - d, ny), wrapped(z0 - s, nz)] = ref[lo : lo + cap, :]


def to_absolute(at, parts, ny, nz, cap):
    vmem = pl.BlockSpec(memory_space=pltpu.VMEM)
    width = parts[0].shape[1]
    return pl.pallas_call(
        functools.partial(to_absolute_kernel, ny, nz, cap),
        out_shape=jax.ShapeDtypeStruct((ny, nz, cap, width), jnp.bfloat16),
        in_specs=[pl.BlockSpec(memory_space=pltpu.SMEM)] + [vmem] * len(parts),
        out_specs=vmem,
        cost_estimate=pl.CostEstimate(
            flops=0, bytes_accessed=4 * ny * nz * cap * width, transcendentals=0
        ),
        compiler_params=pltpu.CompilerParams(vmem_limit_bytes=KERNEL_VMEM),
        name="to_absolute",
    )(at, *parts)


def to_relative_kernel(ny, nz, cap, at_ref, in_ref, out_ref):
    y0, z0 = at_ref[0], at_ref[1]
    lo = 0
    for distances in chunk_sources(nz):
        for d in range(ny):
            for s in distances:
                out_ref[lo : lo + cap, :] = in_ref[wrapped(y0 - d, ny), wrapped(z0 - s, nz)]
                lo += cap


def to_relative(at, a, ny, nz, cap):
    vmem = pl.BlockSpec(memory_space=pltpu.VMEM)
    width = a.shape[-1]
    return pl.pallas_call(
        functools.partial(to_relative_kernel, ny, nz, cap),
        out_shape=jax.ShapeDtypeStruct((ny * nz * cap, width), jnp.bfloat16),
        in_specs=[pl.BlockSpec(memory_space=pltpu.SMEM), vmem],
        out_specs=vmem,
        cost_estimate=pl.CostEstimate(
            flops=0, bytes_accessed=4 * ny * nz * cap * width, transcendentals=0
        ),
        compiler_params=pltpu.CompilerParams(vmem_limit_bytes=KERNEL_VMEM),
        name="to_relative",
    )(at, a.reshape(ny, nz, cap, width))


def shift(a, axis, size, by):
    return lax.ppermute(a, axis, [(i, (i + by) % size) for i in range(size)])


def local(out_grads, route_probs, expert_ids, saved_inputs, w_latent, block_exponents):
    nx, nc, ny, nz = (lax.axis_size(a) for a in ("x", "core", "y", "z"))
    experts = ny * nz
    tok, topk = expert_ids.shape
    feat = out_grads.shape[1]
    hidden = saved_inputs.shape[2]
    cap = tok * topk * 3 // (2 * experts)
    slots = tok * topk
    rows = experts * cap
    at = jnp.stack([lax.axis_index("y"), lax.axis_index("z")]).astype(jnp.int32)

    high = lax.reduce_precision(route_probs, 8, 7)
    rest = route_probs - high
    middle = lax.reduce_precision(rest, 8, 7)
    meta = jnp.concatenate(
        [expert_ids.astype(jnp.float32), high, middle, rest - middle], axis=1
    ).astype(jnp.bfloat16)
    meta = jnp.pad(meta, ((0, 0), (0, META - 4 * topk)))
    own = jnp.concatenate([out_grads, meta], axis=1)

    flat_ids = expert_ids.reshape(slots)
    onehot = flat_ids[:, None] == jnp.arange(experts, dtype=jnp.int32)[None, :]
    tri = (jnp.arange(slots)[:, None] > jnp.arange(slots)[None, :]).astype(jnp.bfloat16)
    before = jnp.dot(tri, onehot.astype(jnp.bfloat16), preferred_element_type=jnp.float32)
    position = jnp.sum(jnp.where(onehot, before, 0.0), axis=1).astype(jnp.int32)
    target = flat_ids * cap + position
    place = (jnp.arange(rows, dtype=jnp.int32)[:, None] == target[None, :]).astype(jnp.bfloat16)

    def exchange(a):
        return lax.all_to_all(
            a.reshape(experts, cap, a.shape[-1]), ("y", "z"), split_axis=0, concat_axis=0, tiled=True
        )

    send_inputs = jnp.dot(
        place, saved_inputs.reshape(slots, hidden), preferred_element_type=jnp.float32
    ).astype(jnp.bfloat16)

    quantized = dequantize(w_latent[0], block_exponents[0])

    share = feat // (nx * nc)
    core, x = lax.axis_index("core"), lax.axis_index("x")
    start = (x * nc + core) * share
    keep_rows = kept(
        (x * nc + core).astype(jnp.int32)[None],
        w_latent[0],
        lax.dynamic_slice_in_dim(block_exponents[0], start, share, 0),
        share,
    )

    got, backs, all_rows = [], [], []

    def deliver(*sources):
        picked = lax.optimization_barrier(pick(at, sources, ny, nz, cap, topk, feat))
        pieces = [picked[0]]
        for d in range(1, ny):
            pieces.append(shift(picked[d], "y", ny, d))
        got.append(pieces)

    def finish(name, *groups):
        group_pieces = [p for g in groups for p in got[g]]
        if name == 0:
            back, here = multiply(group_pieces, quantized)
        else:
            here = jnp.concatenate(group_pieces, axis=0).reshape(-1, feat)
            back = jnp.dot(here, quantized, preferred_element_type=jnp.float32)
            back = back.astype(jnp.bfloat16)
        all_rows.append(here)
        lo = 0
        for g in groups:
            count = sum(p.shape[0] for p in got[g]) * cap
            backs.append(back[lo : lo + count])
            lo += count

    def hop(right, left):
        right = shift(right, "z", nz, 1)
        left = shift(left, "z", nz, -1)
        return right, left

    right, left = hop(own, own)
    right, left, quantized = lax.optimization_barrier((right, left, quantized))
    deliver((own,), (right,), (left,))
    right, left = hop(right, left)
    deliver((right,), (left,))
    right, left = hop(right, left)
    deliver((right,), (left,))
    right, left = hop(right[: tok // 2], left[tok // 2 :])
    got_inputs = exchange(send_inputs)
    deliver((right, left))
    finish(0, 0, 1)
    finish(1, 2, 3)

    back = to_absolute(at, backs, ny, nz, cap)
    returned = exchange(back).reshape(rows, hidden)
    input_grads = jnp.dot(place.T, returned, preferred_element_type=jnp.float32).astype(
        jnp.bfloat16
    )

    all_grads = jnp.concatenate(all_rows, axis=0)

    partial = lax.dot_general(
        all_grads,
        to_relative(at, got_inputs, ny, nz, cap),
        (((0,), (0,)), ((), ())),
        preferred_element_type=jnp.float32,
    ).astype(jnp.bfloat16)
    partial = partial.reshape(nx, nc, share, hidden)
    other = lax.dynamic_index_in_dim(partial, 1 - core, 1, keepdims=False)
    other = shift(other, "core", nc, 1)
    pieces = pieces_of(jnp.stack([x, core]).astype(jnp.int32), partial, other)

    def wide(d, columns=slice(None)):
        return pieces[d % nx, :, columns].astype(jnp.float32)

    low, high = slice(0, hidden // 2), slice(hidden // 2, None)
    up = shift(pieces[2, :, low], "x", nx, 1)
    down = shift(pieces[2, :, high], "x", nx, -1)
    left_high = shift(pieces[1, :, high], "x", nx, 1)
    right_low = shift(pieces[-1, :, low], "x", nx, -1)
    relay_right = (wide(1, low) + up.astype(jnp.float32)).astype(jnp.bfloat16)
    relay_left = (wide(-1, high) + down.astype(jnp.float32)).astype(jnp.bfloat16)
    left_low = shift(relay_right, "x", nx, 1)
    right_high = shift(relay_left, "x", nx, -1)
    from_left = jnp.concatenate([left_low, left_high], axis=1).astype(jnp.float32)
    from_right = jnp.concatenate([right_low, right_high], axis=1).astype(jnp.float32)
    summed = wide(0) + from_left + from_right
    weight_grads = summed * keep_rows.astype(jnp.float32)
    return (input_grads.reshape(tok, topk, hidden), weight_grads[None])


def solution(mesh):
    split = Mesh(mesh.devices.reshape(4, 2, 4, 8), ("x", "core", "y", "z"))
    every = ("x", "core", "y", "z")
    placed = (
        P(every, None),
        P(every, None),
        P(every, None),
        P(every, None, None),
        P(("y", "z"), None, None),
        P(("y", "z"), None, None),
    )
    return jax.shard_map(
        local,
        mesh=split,
        in_specs=placed,
        out_specs=(P(every, None, None), P(("y", "z"), ("x", "core"), None)),
        check_vma=False,
    )
```

```python
import functools

import jax
import jax.numpy as jnp
from jax import lax
from jax.experimental import pallas as pl
from jax.experimental.pallas import tpu as pltpu
from jax.sharding import Mesh, PartitionSpec as P


BLK = 128
KERNEL_VMEM = 20 << 20
META = 128


def dequantize_kernel(weight_ref, exponent_ref, out_ref):
    powers = jnp.left_shift(jnp.ones_like(exponent_ref[...]), -exponent_ref[...])
    powers = powers.astype(jnp.float32).T
    inverses = 1.0 / powers
    center = jnp.bfloat16(192.0)
    for b in range(powers.shape[1]):
        here = slice(b * BLK, (b + 1) * BLK)
        shape = (powers.shape[0], BLK)
        power = jnp.broadcast_to(powers[:, b : b + 1], shape).astype(jnp.bfloat16)
        inverse = jnp.broadcast_to(inverses[:, b : b + 1], shape).astype(jnp.bfloat16)
        shifted = weight_ref[:, here] * power + center
        shifted = jnp.clip(shifted, jnp.bfloat16(184.0), jnp.bfloat16(199.0))
        out_ref[:, here] = (shifted - center) * inverse


def dequantize(weight_one, exponent_one):
    feat, hidden = weight_one.shape
    step = 128
    return pl.pallas_call(
        dequantize_kernel,
        out_shape=jax.ShapeDtypeStruct((feat, hidden), jnp.bfloat16),
        grid=(feat // step,),
        in_specs=[
            pl.BlockSpec((step, hidden), lambda i: (i, 0)),
            pl.BlockSpec((hidden // BLK, step), lambda i: (0, i)),
        ],
        out_specs=pl.BlockSpec((step, hidden), lambda i: (i, 0)),
        cost_estimate=pl.CostEstimate(
            flops=12 * feat * hidden, bytes_accessed=4 * feat * hidden, transcendentals=0
        ),
        compiler_params=pltpu.CompilerParams(vmem_limit_bytes=KERNEL_VMEM),
        name="dequantize",
    )(weight_one, exponent_one.T)


def kept_kernel(at_ref, weight_ref, exponent_ref, out_ref):
    powers = jnp.left_shift(jnp.ones_like(exponent_ref[...]), -exponent_ref[...])
    powers = powers.astype(jnp.float32)
    for b in range(powers.shape[1]):
        here = slice(b * BLK, (b + 1) * BLK)
        codes = weight_ref[:, here].astype(jnp.float32) * powers[:, b : b + 1]
        inside = jnp.where(codes >= -8.5, jnp.where(codes <= 7.5, 1.0, 0.0), 0.0)
        out_ref[:, here] = inside.astype(jnp.bfloat16)


def kept(block, weight_one, exponents, share):
    hidden = weight_one.shape[1]
    parts = 7
    step = share // parts
    return pl.pallas_call(
        kept_kernel,
        out_shape=jax.ShapeDtypeStruct((share, hidden), jnp.bfloat16),
        grid_spec=pltpu.PrefetchScalarGridSpec(
            num_scalar_prefetch=1,
            grid=(parts,),
            in_specs=[
                pl.BlockSpec((step, hidden), lambda i, at: (at[0] * parts + i, 0)),
                pl.BlockSpec((step, hidden // BLK), lambda i, at: (i, 0)),
            ],
            out_specs=pl.BlockSpec((step, hidden), lambda i, at: (i, 0)),
        ),
        cost_estimate=pl.CostEstimate(
            flops=4 * share * hidden, bytes_accessed=4 * share * hidden, transcendentals=0
        ),
        compiler_params=pltpu.CompilerParams(vmem_limit_bytes=KERNEL_VMEM),
        name="kept",
    )(block, weight_one, exponents)


def pieces_kernel(at_ref, mine_ref, other_ref, out_ref):
    total = mine_ref[0, 0].astype(jnp.float32) + other_ref[0].astype(jnp.float32)
    out_ref[0] = total.astype(jnp.bfloat16)


def pieces_of(at, partial, other):
    nx, _, share, width = partial.shape
    return pl.pallas_call(
        pieces_kernel,
        out_shape=jax.ShapeDtypeStruct((nx, share, width), jnp.bfloat16),
        grid_spec=pltpu.PrefetchScalarGridSpec(
            num_scalar_prefetch=1,
            grid=(nx,),
            in_specs=[
                pl.BlockSpec(
                    (1, 1, share, width), lambda d, at: (lax.rem(at[0] + d, nx), at[1], 0, 0)
                ),
                pl.BlockSpec((1, share, width), lambda d, at: (lax.rem(at[0] + d, nx), 0, 0)),
            ],
            out_specs=pl.BlockSpec((1, share, width), lambda d, at: (d, 0, 0)),
        ),
        cost_estimate=pl.CostEstimate(
            flops=nx * share * width, bytes_accessed=6 * nx * share * width, transcendentals=0
        ),
        name="pieces",
    )(at, partial, other)


def pick_kernel(ny, nz, cap, topk, feat, shape, at_ref, *refs):
    refs, outs = refs[:-ny], refs[-ny:]
    sources, lo = [], 0
    for parts in shape:
        sources.append(refs[lo : lo + parts])
        lo += parts
    tok = sum(r.shape[0] for r in sources[0])
    y0, z0 = at_ref[0], at_ref[1]

    def split(j):
        g = jnp.zeros_like(j)
        for d in range(1, ny):
            g = g + (j >= d * cap).astype(jnp.int32)
        return g, j - g * cap

    def expert(g):
        y = y0 + g
        return (jnp.where(y >= ny, y - ny, y) * nz + z0).astype(jnp.float32)

    lane = lax.broadcasted_iota(jnp.int32, (tok, META), 1)
    group, slot = split(lane)
    lane_expert, lane_slot = expert(group), slot.astype(jnp.float32)
    row_expert = expert(split(lax.broadcasted_iota(jnp.int32, (META, META), 0))[0])[:, :1]
    earlier = (
        lax.broadcasted_iota(jnp.int32, (tok, tok), 1)
        < lax.broadcasted_iota(jnp.int32, (tok, tok), 0)
    )
    earlier = earlier.astype(jnp.float32).astype(jnp.bfloat16)

    for i, parts in enumerate(sources):

        def columns(lo, hi):
            got = [p[:, lo:hi] for p in parts]
            return got[0] if len(got) == 1 else jnp.concatenate(got, axis=0)

        meta_low = columns(feat, feat + META)
        meta = meta_low.astype(jnp.float32)
        hit = jnp.zeros((tok, META), jnp.float32)
        for k in range(topk):
            hit = jnp.where(meta[:, k : k + 1] == lane_expert, 1.0, hit)
        hit = jnp.where(lane < ny * cap, hit, 0.0)
        before = jnp.dot(earlier, hit.astype(jnp.bfloat16), preferred_element_type=jnp.float32)
        chosen = jnp.where(before == lane_slot, hit, 0.0)
        chosen = chosen.T.astype(jnp.bfloat16)
        info = jnp.dot(chosen, meta_low, preferred_element_type=jnp.float32)
        prob = jnp.zeros((META, 1), jnp.float32)
        for k in range(topk):
            value = info[:, topk + k : topk + k + 1]
            value = value + info[:, 2 * topk + k : 2 * topk + k + 1]
            value = value + info[:, 3 * topk + k : 3 * topk + k + 1]
            prob = jnp.where(info[:, k : k + 1] == row_expert, value, prob)
        step = 512
        for lo in range(0, feat, step):
            rows = jnp.dot(chosen, columns(lo, lo + step), preferred_element_type=jnp.float32)
            rows = rows * prob
            for d in range(ny):
                outs[d][i, :, lo : lo + step] = rows[d * cap : (d + 1) * cap].astype(jnp.bfloat16)


def pick(at, sources, ny, nz, cap, topk, feat):
    count = len(sources)
    shape = tuple(len(parts) for parts in sources)
    tok = sum(p.shape[0] for p in sources[0])
    flat = [p for parts in sources for p in parts]
    vmem = pl.BlockSpec(memory_space=pltpu.VMEM)
    return pl.pallas_call(
        functools.partial(pick_kernel, ny, nz, cap, topk, feat, shape),
        out_shape=[jax.ShapeDtypeStruct((count, cap, feat), jnp.bfloat16)] * ny,
        in_specs=[pl.BlockSpec(memory_space=pltpu.SMEM)] + [vmem] * len(flat),
        out_specs=[vmem] * ny,
        cost_estimate=pl.CostEstimate(
            flops=2 * count * META * tok * feat,
            bytes_accessed=2 * count * (tok + ny * cap) * feat,
            transcendentals=0,
        ),
        compiler_params=pltpu.CompilerParams(vmem_limit_bytes=KERNEL_VMEM),
    )(at, *flat)


def wrapped(a, size):
    return jnp.where(a >= size, a - size, jnp.where(a < 0, a + size, a))


def chunk_sources(nz):
    return [[0, 1, -1]] + [[s, -s] for s in range(2, nz // 2)] + [[nz // 2]]


def multiply_kernel(*refs):
    pieces, (weight_ref, out_ref, rows_ref, acc_ref) = refs[:-4], refs[-4:]
    i = pl.program_id(0)
    rows = [p[c] for p in pieces for c in range(p.shape[0])]
    here = jnp.concatenate(rows, axis=0)
    rows_ref[...] = here
    part = jnp.dot(here, weight_ref[...], preferred_element_type=jnp.float32)

    @pl.when(i == 0)
    def _():
        acc_ref[...] = part

    @pl.when(i > 0)
    def _():
        acc_ref[...] += part

    @pl.when(i == pl.num_programs(0) - 1)
    def _():
        out_ref[...] = acc_ref[...].astype(jnp.bfloat16)


def multiply(pieces, weight):
    cap, feat = pieces[0].shape[1:]
    rows, hidden, step = sum(p.shape[0] for p in pieces) * cap, weight.shape[1], 512
    return pl.pallas_call(
        multiply_kernel,
        out_shape=[
            jax.ShapeDtypeStruct((rows, hidden), jnp.bfloat16),
            jax.ShapeDtypeStruct((rows, feat), jnp.bfloat16),
        ],
        grid=(feat // step,),
        in_specs=[pl.BlockSpec((p.shape[0], cap, step), lambda i: (0, 0, i)) for p in pieces]
        + [pl.BlockSpec((step, hidden), lambda i: (i, 0))],
        out_specs=[
            pl.BlockSpec((rows, hidden), lambda i: (0, 0)),
            pl.BlockSpec((rows, step), lambda i: (0, i)),
        ],
        scratch_shapes=[pltpu.VMEM((rows, hidden), jnp.float32)],
        cost_estimate=pl.CostEstimate(
            flops=2 * rows * feat * hidden,
            bytes_accessed=2 * feat * (rows + hidden),
            transcendentals=0,
        ),
        name="multiply",
    )(*pieces, weight)


def to_absolute_kernel(ny, nz, cap, at_ref, *refs):
    out_ref = refs[-1]
    y0, z0 = at_ref[0], at_ref[1]
    for ref, distances in zip(refs[:-1], chunk_sources(nz), strict=True):
        for d in range(ny):
            for i, s in enumerate(distances):
                lo = (d * len(distances) + i) * cap
                out_ref[wrapped(y0 - d, ny), wrapped(z0 - s, nz)] = ref[lo : lo + cap, :]


def to_absolute(at, parts, ny, nz, cap):
    vmem = pl.BlockSpec(memory_space=pltpu.VMEM)
    width = parts[0].shape[1]
    return pl.pallas_call(
        functools.partial(to_absolute_kernel, ny, nz, cap),
        out_shape=jax.ShapeDtypeStruct((ny, nz, cap, width), jnp.bfloat16),
        in_specs=[pl.BlockSpec(memory_space=pltpu.SMEM)] + [vmem] * len(parts),
        out_specs=vmem,
        cost_estimate=pl.CostEstimate(
            flops=0, bytes_accessed=4 * ny * nz * cap * width, transcendentals=0
        ),
        compiler_params=pltpu.CompilerParams(vmem_limit_bytes=KERNEL_VMEM),
        name="to_absolute",
    )(at, *parts)


def to_relative_kernel(ny, nz, cap, at_ref, in_ref, out_ref):
    y0, z0 = at_ref[0], at_ref[1]
    lo = 0
    for distances in chunk_sources(nz):
        for d in range(ny):
            for s in distances:
                out_ref[lo : lo + cap, :] = in_ref[wrapped(y0 - d, ny), wrapped(z0 - s, nz)]
                lo += cap


def to_relative(at, a, ny, nz, cap):
    vmem = pl.BlockSpec(memory_space=pltpu.VMEM)
    width = a.shape[-1]
    return pl.pallas_call(
        functools.partial(to_relative_kernel, ny, nz, cap),
        out_shape=jax.ShapeDtypeStruct((ny * nz * cap, width), jnp.bfloat16),
        in_specs=[pl.BlockSpec(memory_space=pltpu.SMEM), vmem],
        out_specs=vmem,
        cost_estimate=pl.CostEstimate(
            flops=0, bytes_accessed=4 * ny * nz * cap * width, transcendentals=0
        ),
        compiler_params=pltpu.CompilerParams(vmem_limit_bytes=KERNEL_VMEM),
        name="to_relative",
    )(at, a.reshape(ny, nz, cap, width))


def shift(a, axis, size, by):
    return lax.ppermute(a, axis, [(i, (i + by) % size) for i in range(size)])


def local(out_grads, route_probs, expert_ids, saved_inputs, w_latent, block_exponents):
    nx, nc, ny, nz = (lax.axis_size(a) for a in ("x", "core", "y", "z"))
    experts = ny * nz
    tok, topk = expert_ids.shape
    feat = out_grads.shape[1]
    hidden = saved_inputs.shape[2]
    cap = tok * topk * 3 // (2 * experts)
    slots = tok * topk
    rows = experts * cap
    at = jnp.stack([lax.axis_index("y"), lax.axis_index("z")]).astype(jnp.int32)

    high = lax.reduce_precision(route_probs, 8, 7)
    rest = route_probs - high
    middle = lax.reduce_precision(rest, 8, 7)
    meta = jnp.concatenate(
        [expert_ids.astype(jnp.float32), high, middle, rest - middle], axis=1
    ).astype(jnp.bfloat16)
    meta = jnp.pad(meta, ((0, 0), (0, META - 4 * topk)))
    own = jnp.concatenate([out_grads, meta], axis=1)

    flat_ids = expert_ids.reshape(slots)
    onehot = flat_ids[:, None] == jnp.arange(experts, dtype=jnp.int32)[None, :]
    tri = (jnp.arange(slots)[:, None] > jnp.arange(slots)[None, :]).astype(jnp.bfloat16)
    before = jnp.dot(tri, onehot.astype(jnp.bfloat16), preferred_element_type=jnp.float32)
    position = jnp.sum(jnp.where(onehot, before, 0.0), axis=1).astype(jnp.int32)
    target = flat_ids * cap + position
    place = (jnp.arange(rows, dtype=jnp.int32)[:, None] == target[None, :]).astype(jnp.bfloat16)

    def exchange(a):
        return lax.all_to_all(
            a.reshape(experts, cap, a.shape[-1]), ("y", "z"), split_axis=0, concat_axis=0, tiled=True
        )

    send_inputs = jnp.dot(
        place, saved_inputs.reshape(slots, hidden), preferred_element_type=jnp.float32
    ).astype(jnp.bfloat16)

    quantized = dequantize(w_latent[0], block_exponents[0])

    share = feat // (nx * nc)
    core, x = lax.axis_index("core"), lax.axis_index("x")
    start = (x * nc + core) * share
    keep_rows = kept(
        (x * nc + core).astype(jnp.int32)[None],
        w_latent[0],
        lax.dynamic_slice_in_dim(block_exponents[0], start, share, 0),
        share,
    )

    got, backs, all_rows = [], [], []

    def deliver(*sources):
        picked = lax.optimization_barrier(pick(at, sources, ny, nz, cap, topk, feat))
        pieces = [picked[0]]
        for d in range(1, ny):
            pieces.append(shift(picked[d], "y", ny, d))
        got.append(pieces)

    def finish(name, *groups):
        group_pieces = [p for g in groups for p in got[g]]
        if name < 2:
            back, here = multiply(group_pieces, quantized)
        else:
            here = jnp.concatenate(group_pieces, axis=0).reshape(-1, feat)
            back = jnp.dot(here, quantized, preferred_element_type=jnp.float32)
            back = back.astype(jnp.bfloat16)
        all_rows.append(here)
        lo = 0
        for g in groups:
            count = sum(p.shape[0] for p in got[g]) * cap
            backs.append(back[lo : lo + count])
            lo += count

    def hop(right, left):
        right = shift(right, "z", nz, 1)
        left = shift(left, "z", nz, -1)
        return right, left

    right, left = hop(own, own)
    right, left, quantized = lax.optimization_barrier((right, left, quantized))
    deliver((own,), (right,), (left,))
    right, left = hop(right, left)
    deliver((right,), (left,))
    right, left = hop(right, left)
    deliver((right,), (left,))
    right, left = hop(right[: tok // 2], left[tok // 2 :])
    got_inputs = exchange(send_inputs)
    deliver((right, left))
    finish(0, 0)
    finish(1, 1, 2)
    finish(2, 3)

    back = to_absolute(at, backs, ny, nz, cap)
    back, got_inputs = lax.optimization_barrier((back, got_inputs))
    returned = exchange(back).reshape(rows, hidden)
    input_grads = jnp.dot(place.T, returned, preferred_element_type=jnp.float32).astype(
        jnp.bfloat16
    )

    all_grads = jnp.concatenate(all_rows, axis=0)

    partial = lax.dot_general(
        all_grads,
        to_relative(at, got_inputs, ny, nz, cap),
        (((0,), (0,)), ((), ())),
        preferred_element_type=jnp.float32,
    ).astype(jnp.bfloat16)
    partial = partial.reshape(nx, nc, share, hidden)
    other = lax.dynamic_index_in_dim(partial, 1 - core, 1, keepdims=False)
    other = shift(other, "core", nc, 1)
    pieces = pieces_of(jnp.stack([x, core]).astype(jnp.int32), partial, other)

    def wide(d, columns=slice(None)):
        return pieces[d % nx, :, columns].astype(jnp.float32)

    low, high = slice(0, hidden // 2), slice(hidden // 2, None)
    up = shift(pieces[2, :, low], "x", nx, 1)
    down = shift(pieces[2, :, high], "x", nx, -1)
    left_high = shift(pieces[1, :, high], "x", nx, 1)
    right_low = shift(pieces[-1, :, low], "x", nx, -1)
    relay_right = (wide(1, low) + up.astype(jnp.float32)).astype(jnp.bfloat16)
    relay_left = (wide(-1, high) + down.astype(jnp.float32)).astype(jnp.bfloat16)
    left_low = shift(relay_right, "x", nx, 1)
    right_high = shift(relay_left, "x", nx, -1)
    from_left = jnp.concatenate([left_low, left_high], axis=1).astype(jnp.float32)
    from_right = jnp.concatenate([right_low, right_high], axis=1).astype(jnp.float32)
    summed = wide(0) + from_left + from_right
    weight_grads = summed * keep_rows.astype(jnp.float32)
    return (input_grads.reshape(tok, topk, hidden), weight_grads[None])


def solution(mesh):
    split = Mesh(mesh.devices.reshape(4, 2, 4, 8), ("x", "core", "y", "z"))
    every = ("x", "core", "y", "z")
    placed = (
        P(every, None),
        P(every, None),
        P(every, None),
        P(every, None, None),
        P(("y", "z"), None, None),
        P(("y", "z"), None, None),
    )
    return jax.shard_map(
        local,
        mesh=split,
        in_specs=placed,
        out_specs=(P(every, None, None), P(("y", "z"), ("x", "core"), None)),
        check_vma=False,
    )
```
